32 devices in a mesh: row: 8 (over z, y), col: 4 (over x, core).
Axes of the slice: x: 2, y: 2, z: 4, core: 2. Of those that a mesh axis runs over, the one named last changes fastest.
Arguments:
- tensor_ri: bfloat16 [8, 8, 4, 128, 1152], P('row', None, 'col'), may hold values from -6 to 6
- block_mask: int32 [8, 4, 9], P('row', 'col'), may hold values 0 or 1
- green_virt: bfloat16 [8, 4, 128, 3200], P('row', 'col'), may hold values from -0.1875 to 0.1875
- green_occ: bfloat16 [8, 4, 128, 128], P('row', 'col'), may hold values from -0.5 to 0.5
Outputs:
- response: float32 [8, 8], replicated
The draws below stay inside these ranges and needn't reach their ends.
All inputs are finite; a program needn't handle non-finite values. No bound on the sum of `block_mask` on one device may be relied on, other than what follows from the above.
Results may differ from the reference program's by a relative error of at most 0.0044.
Values may be sent and summed in bfloat16 or wider, within the bound.
A program may use at most 192 MiB of HBM per device.

```python
import math
import jax
import jax.numpy as jnp
from jax import lax

BLK = 128
NP = 8
AO = 4096
N_ROW = 8
N_COL = 4


def place_ends(entries, key, low, top_value):
    place = [jax.random.randint(jax.random.fold_in(key, axis), (), 0, length) for axis, length in enumerate(entries.shape)]
    main_axis = entries.shape.index(max(entries.shape))
    beside = place[:main_axis] + [(place[main_axis] + 1) % entries.shape[main_axis]] + place[main_axis + 1:]
    return entries.at[tuple(place)].set(low).at[tuple(beside)].set(top_value)


def levels(key, shape, split, low, top_value):
    factor_of = 1.0
    for position, blocks in split:
        heights = jax.random.uniform(jax.random.fold_in(jax.random.fold_in(key, 6), position), (blocks,), jnp.float32, low / len(split), top_value / len(split))
        factor_of = factor_of * jnp.repeat(jnp.exp(heights), shape[position] // blocks).reshape((-1,) + (1,) * (len(shape) - 1 - position))
    return factor_of


def gaussian(own_key, extent, deviation, reach, cuts=(), kind=jnp.bfloat16):
    loudness = levels(own_key, extent, cuts, -0.22, 0.18) if cuts else 1.0
    array = jax.random.normal(own_key, extent, jnp.float32) * deviation * loudness
    return jnp.minimum(jnp.maximum(array, -reach), reach).astype(kind)


def setup_inputs(seed: int = 0) -> dict:
    key_of = jax.random.split(jax.random.key(seed), 5)
    tensor_ri = gaussian(key_of[0], (NP, N_ROW, N_COL, BLK, 9 * BLK), 1.0, 6.0, ((0, 8), (2, 4)))
    block_mask = place_ends((jax.random.randint(key_of[1], (N_ROW, N_COL, 9), 0, 4) < 3).astype(jnp.int32), jax.random.fold_in(key_of[1], 1), 0, 1)
    green_virt = gaussian(key_of[2], (N_ROW, N_COL, BLK, 25 * BLK), (9 * BLK) ** -0.5, 0.1875, ((0, 8), (1, 4)))
    green_occ = gaussian(key_of[3], (N_ROW, N_COL, BLK, BLK), BLK ** -0.5, 0.5, ((0, 8), (1, 4)))
    return dict(tensor_ri=tensor_ri, block_mask=block_mask, green_virt=green_virt, green_occ=green_occ)


def assemble(rim_blocks, block_width):
    rows_list = []
    for source in range(9):
        src_row, src_col = (source // 3, source % 3)
        pieces = []
        for target in range(9):
            tgt_row, tgt_col = (target // 3, target % 3)
            band_slot = (tgt_row - src_row + 2) * 5 + (tgt_col - src_col + 2)
            pieces.append(rim_blocks[src_row, src_col, :, band_slot * block_width:(band_slot + 1) * block_width])
        rows_list.append(jnp.concatenate(pieces, axis=1))
    return jnp.concatenate(rows_list, axis=0)

def reference(tensor_ri, block_mask, green_virt, green_occ):
    pair_width = 9 * BLK
    padded_green = jnp.pad(green_virt, ((1, 1), (1, 1), (0, 0), (0, 0)))
    slots = jnp.arange(9, dtype=jnp.int32)

    def accumulate(total, index):
        grid_row = (index // N_COL).astype(jnp.int32)
        grid_col = (index % N_COL).astype(jnp.int32)
        zero = jnp.zeros((), jnp.int32)
        tensor_block = lax.dynamic_slice(tensor_ri, (zero, grid_row, grid_col, zero, zero), (NP, 1, 1, BLK, pair_width))
        tensor_block = tensor_block.reshape(NP, BLK, pair_width)
        slot_mask = lax.dynamic_slice(block_mask, (grid_row, grid_col, zero), (1, 1, 9)).reshape(9)
        near_row = grid_row + slots // 3 - 1
        near_col = grid_col + slots % 3 - 1
        usable = (slot_mask == 1) & (near_row >= 0) & (near_row < N_ROW) & (near_col >= 0) & (near_col < N_COL)
        kept_slots = jnp.repeat(usable.astype(tensor_block.dtype), BLK)
        tensor_block = tensor_block * kept_slots
        rim_blocks = lax.dynamic_slice(padded_green, (grid_row, grid_col, zero, zero), (3, 3, BLK, 25 * BLK))
        green_pairs = assemble(rim_blocks, BLK)
        half_done = jnp.dot(tensor_block.reshape(NP * BLK, pair_width), green_pairs, preferred_element_type=jnp.float32)
        half_done = half_done.astype(jnp.bfloat16).reshape(NP, BLK * pair_width)
        occ_block = lax.dynamic_slice(green_occ, (grid_row, grid_col, zero, zero), (1, 1, BLK, BLK)).reshape(BLK, BLK)
        occ_applied = jnp.einsum('ji,pik->pjk', occ_block.astype(jnp.float32), tensor_block.astype(jnp.float32))
        occ_applied = occ_applied.astype(jnp.bfloat16).reshape(NP, BLK * pair_width)
        product = lax.dot_general(half_done, occ_applied, (((1,), (1,)), ((), ())), preferred_element_type=jnp.float32)
        return (total + product, None)
    start = jnp.zeros((NP, NP), jnp.float32)
    total, unused = lax.scan(accumulate, start, jnp.arange(N_ROW * N_COL, dtype=jnp.int32))
    return total * (1.0 / math.sqrt(AO * 9 * BLK))
```

```python
import functools
import math

import jax
import jax.numpy as jnp
from jax import lax
from jax.experimental import pallas as pl
from jax.experimental.pallas import tpu as pltpu
from jax.sharding import PartitionSpec as P

MESH = pl.DeviceIdType.MESH
NT = (((1,), (1,)), ((), ()))


def kernel(rows, cols, width, scale, mask_ref, occ_ref, tensor_ref, green_ref, out_ref,
           held, half, pairs, part, row_sums, col_sums,
           own_sem, own_green_sem, send_sem, recv_sem, green_send, green_recv,
           row_send, row_recv, col_send, col_recv):
    r = lax.axis_index("row")
    c = lax.axis_index("col")
    bits = (rows - 1).bit_length()

    def partner(step):
        other = 0
        for bit in range(bits):
            other = other + (1 << bit) * ((r // (1 << bit) + step // (1 << bit)) % 2)
        return other

    def at_lane(block):
        return pl.multiple_of(block * width, width)

    def spans(col, fn):
        inner = (col > 0) & (col < cols - 1)

        @pl.when(inner)
        def _():
            fn(0, 3)

        @pl.when(col == 0)
        def _():
            fn(1, 2)

        @pl.when(col == cols - 1)
        def _():
            fn(0, 2)

    def tensor_copy(src_row, dst_row, step, a, first, count):
        lanes = pl.ds((3 * a + first) * width, count * width)
        return pltpu.make_async_remote_copy(
            src_ref=tensor_ref.at[0, dst_row, 0, :, lanes],
            dst_ref=held.at[src_row, :, lanes],
            send_sem=send_sem.at[step, a],
            recv_sem=recv_sem.at[step, a],
            device_id=(dst_row, c),
            device_id_type=MESH,
        )

    def green_copy(ap, bp, a, first, count, target):
        slot = 3 * ap + bp
        band = 5 * (a - ap + 2) + (first - bp + 2)
        return pltpu.make_async_remote_copy(
            src_ref=green_ref.at[0, 0, :, pl.ds(band * width, count * width)],
            dst_ref=pairs.at[pl.ds(slot * width, width), pl.ds((3 * a + first) * width, count * width)],
            send_sem=green_send.at[slot, a],
            recv_sem=green_recv.at[slot, a],
            device_id=target,
            device_id_type=MESH,
        )

    def row_ok(row):
        return (row >= 0) & (row < rows)

    def col_ok(col):
        return (col >= 0) & (col < cols)

    def each_green_sent(fn):
        for ap in range(3):
            for bp in range(3):
                if ap == 1 and bp == 1:
                    continue
                to_row, to_col = r + 1 - ap, c + 1 - bp

                @pl.when(row_ok(to_row) & col_ok(to_col))
                def _():
                    for a in range(3):
                        @pl.when(row_ok(to_row + a - 1))
                        def _():
                            spans(to_col, lambda first, count: fn(
                                green_copy(ap, bp, a, first, count, (to_row, to_col))))

    def each_green_received(fn):
        for ap in range(3):
            for bp in range(3):
                if ap == 1 and bp == 1:
                    continue

                @pl.when(row_ok(r + ap - 1) & col_ok(c + bp - 1))
                def _():
                    for a in range(3):
                        @pl.when(row_ok(r + a - 1))
                        def _():
                            spans(c, lambda first, count: fn(
                                green_copy(ap, bp, a, first, count, (r, c))))

    def each_tensor_sent(step, fn):
        other = partner(step)
        for a in range(3):
            @pl.when(row_ok(other + a - 1))
            def _():
                spans(c, lambda first, count: fn(tensor_copy(r, other, step, a, first, count)))

    def each_tensor_received(step, fn):
        other = partner(step)
        for a in range(3):
            @pl.when(row_ok(r + a - 1))
            def _():
                spans(c, lambda first, count: fn(tensor_copy(other, r, step, a, first, count)))

    own = pltpu.make_async_copy(tensor_ref.at[0, r, 0], held.at[r], own_sem)
    own.start()
    own_green = []
    for a in range(3):
        band = 5 * (a + 1) + 1
        own_green.append(pltpu.make_async_copy(
            green_ref.at[0, 0, :, pl.ds(band * width, 3 * width)],
            pairs.at[pl.ds(4 * width, width), pl.ds(3 * a * width, 3 * width)],
            own_green_sem.at[a]))
        own_green[a].start()

    barrier = pltpu.get_barrier_semaphore()

    def greet(row, col):
        pl.semaphore_signal(barrier, inc=1, device_id=(row, col), device_id_type=MESH)

    @pl.loop(1, rows)
    def _(step):
        greet(partner(step), c)

    @pl.loop(1, cols)
    def _(step):
        greet(r, (c + step) % cols)

    corners = 0
    for dr in (-1, 1):
        for dc in (-1, 1):
            there = row_ok(r + dr) & col_ok(c + dc)
            corners = corners + there.astype(jnp.int32)

            @pl.when(there)
            def _():
                greet(r + dr, c + dc)

    pl.semaphore_wait(barrier, rows - 1 + cols - 1 + corners)

    each_green_sent(lambda copy: copy.start())

    @pl.loop(1, rows)
    def _(step):
        each_tensor_sent(rows - step, lambda copy: copy.start())

    @pl.loop(1, rows)
    def _(step):
        other = partner(step)
        for a in range(3):
            for b in range(3):
                @pl.when(jnp.logical_not(row_ok(r + a - 1) & col_ok(c + b - 1)))
                def _():
                    held[other, :, pl.ds((3 * a + b) * width, width)] = jnp.zeros((width, width), held.dtype)

    for copy in own_green:
        copy.wait()
    each_green_received(lambda copy: copy.wait_recv())

    keep = []
    for k in range(9):
        a, b = k // 3, k % 3
        inside = (row_ok(r + a - 1) & col_ok(c + b - 1)).astype(jnp.int32)
        keep.append((mask_ref[0, 0, k] == 1).astype(jnp.int32) * inside)
    for kp in range(9):
        for k in range(9):
            both = jnp.full((width, width), keep[kp] * keep[k], jnp.int32)
            tile = pairs[kp * width:(kp + 1) * width, k * width:(k + 1) * width].astype(jnp.float32)
            pairs[kp * width:(kp + 1) * width, k * width:(k + 1) * width] = jnp.where(
                both == 1, tile, 0.0).astype(pairs.dtype)

    own.wait()
    occ = occ_ref[0, 0].astype(jnp.float32)

    def pair_row(left, right):
        gram = lax.dot_general(half[left], held[right], NT, preferred_element_type=jnp.float32)
        return jnp.sum(gram * occ, axis=0, keepdims=True)

    @pl.loop(0, rows)
    def _(step):
        p = partner(step)

        @pl.when(step > 0)
        def _():
            each_tensor_received(step, lambda copy: copy.wait_recv())

        for a in range(3):
            lanes = slice(3 * a * width, 3 * (a + 1) * width)
            half[p, :, lanes] = jnp.dot(
                held[p], pairs[:, lanes], preferred_element_type=jnp.float32).astype(half.dtype)

        @pl.loop(0, step + 1)
        def _(earlier):
            q = partner(earlier)
            part[p, pl.ds(q, 1), :] = pair_row(p, q)
            part[q, pl.ds(p, 1), :] = pair_row(q, p)

    lanes_total = row_sums.shape[-1]
    row_sums[r] = jnp.zeros(row_sums.shape[1:], jnp.float32)
    row_sums[r, :, 0:rows] = jnp.sum(part[...], axis=2)

    def row_copy(step, src, dst):
        return pltpu.make_async_remote_copy(
            src_ref=row_sums.at[src], dst_ref=row_sums.at[src],
            send_sem=row_send.at[step], recv_sem=row_recv.at[step],
            device_id=(dst, c), device_id_type=MESH)

    def col_copy(step, src, dst):
        return pltpu.make_async_remote_copy(
            src_ref=col_sums.at[src], dst_ref=col_sums.at[src],
            send_sem=col_send.at[step], recv_sem=col_recv.at[step],
            device_id=(r, dst), device_id_type=MESH)

    @pl.loop(1, rows)
    def _(step):
        row_copy(step, r, partner(step)).start()

    @pl.loop(1, rows)
    def _(step):
        row_copy(step, partner(step), r).wait_recv()

    col_sums[c] = jnp.sum(row_sums[...], axis=0)

    @pl.loop(1, cols)
    def _(step):
        col_copy(step, c, (c + step) % cols).start()

    @pl.loop(1, cols)
    def _(step):
        col_copy(step, (c + cols - step) % cols, c).wait_recv()

    out_ref[...] = (jnp.sum(col_sums[...], axis=0) * scale)[:, 0:rows]

    each_green_sent(lambda copy: copy.wait_send())

    @pl.loop(1, rows)
    def _(step):
        each_tensor_sent(step, lambda copy: copy.wait_send())
        row_copy(step, r, partner(step)).wait_send()

    @pl.loop(1, cols)
    def _(step):
        col_copy(step, c, (c + step) % cols).wait_send()


def per_device(tensor_ri, block_mask, green_virt, green_occ):
    rows = lax.axis_size("row")
    cols = lax.axis_size("col")
    width = green_occ.shape[-1]
    wide = tensor_ri.shape[-1]
    scale = 1.0 / math.sqrt(width * rows * cols * wide)
    lanes = 128
    hbm = pl.BlockSpec(memory_space=pltpu.MemorySpace.HBM)
    dma = pltpu.SemaphoreType.DMA
    return pl.pallas_call(
        functools.partial(kernel, rows, cols, width, scale),
        out_shape=jax.ShapeDtypeStruct((rows, rows), jnp.float32),
        in_specs=[
            pl.BlockSpec(memory_space=pltpu.MemorySpace.SMEM),
            pl.BlockSpec(memory_space=pltpu.MemorySpace.VMEM),
            hbm,
            hbm,
        ],
        out_specs=pl.BlockSpec(memory_space=pltpu.MemorySpace.VMEM),
        scratch_shapes=[
            pltpu.VMEM((rows, width, wide), jnp.bfloat16),
            pltpu.VMEM((rows, width, wide), jnp.bfloat16),
            pltpu.VMEM((wide, wide), jnp.bfloat16),
            pltpu.VMEM((rows, rows, width), jnp.float32),
            pltpu.VMEM((rows, rows, lanes), jnp.float32),
            pltpu.VMEM((cols, rows, lanes), jnp.float32),
            dma,
            dma((3,)),
            dma((rows, 3)),
            dma((rows, 3)),
            dma((9, 3)),
            dma((9, 3)),
            dma((rows,)),
            dma((rows,)),
            dma((cols,)),
            dma((cols,)),
        ],
        compiler_params=pltpu.CompilerParams(
            collective_id=0, has_side_effects=True, vmem_limit_bytes=63 * 1024 * 1024),
    )(block_mask, green_occ, tensor_ri, green_virt)


def solution(mesh):
    return jax.shard_map(
        per_device,
        mesh=mesh,
        in_specs=(
            P("row", None, "col", None, None),
            P("row", "col", None),
            P("row", "col", None, None),
            P("row", "col", None, None),
        ),
        out_specs=P(),
        check_vma=False,
    )
```

```python
import functools
import math

import jax
import jax.numpy as jnp
from jax import lax
from jax.experimental import pallas as pl
from jax.experimental.pallas import tpu as pltpu
from jax.sharding import PartitionSpec as P

MESH = pl.DeviceIdType.MESH
NT = (((1,), (1,)), ((), ()))


def kernel(rows, cols, width, scale, mask_ref, occ_ref, tensor_ref, green_ref, out_ref,
           held, half, pairs, stage, part, row_sums, col_sums,
           own_sem, own_green_sem, send_sem, recv_sem, green_send, green_recv,
           stage_send, stage_recv, forward_send,
           row_send, row_recv, col_send, col_recv):
    r = lax.axis_index("row")
    c = lax.axis_index("col")
    bits = (rows - 1).bit_length()
    wide = 9 * width

    def partner(step):
        other = 0
        for bit in range(bits):
            other = other + (1 << bit) * ((r // (1 << bit) + step // (1 << bit)) % 2)
        return other

    def at_lane(block):
        return pl.multiple_of(block * width, width)

    def spans(col, fn):
        inner = (col > 0) & (col < cols - 1)

        @pl.when(inner)
        def _():
            fn(0, 3)

        @pl.when(col == 0)
        def _():
            fn(1, 2)

        @pl.when(col == cols - 1)
        def _():
            fn(0, 2)

    def tensor_copy(src_row, dst_row, step, a, first, count):
        lanes = pl.ds((3 * a + first) * width, count * width)
        return pltpu.make_async_remote_copy(
            src_ref=tensor_ref.at[0, dst_row, 0, :, lanes],
            dst_ref=held.at[step, :, lanes],
            send_sem=send_sem.at[step, a],
            recv_sem=recv_sem.at[step, a],
            device_id=(dst_row, c),
            device_id_type=MESH,
        )

    def green_copy(ap, bp, a, first, count, target):
        slot = 3 * ap + bp
        band = 5 * (a - ap + 2) + (first - bp + 2)
        return pltpu.make_async_remote_copy(
            src_ref=green_ref.at[0, 0, :, pl.ds(band * width, count * width)],
            dst_ref=pairs.at[pl.ds(slot * width, width), pl.ds((3 * a + first) * width, count * width)],
            send_sem=green_send.at[slot, a],
            recv_sem=green_recv.at[slot, a],
            device_id=target,
            device_id_type=MESH,
        )

    def row_ok(row):
        return (row >= 0) & (row < rows)

    def col_ok(col):
        return (col >= 0) & (col < cols)

    def each_green_sent(fn):
        for ap in range(3):
            for bp in range(3):
                if ap == 1 and bp == 1:
                    continue
                to_row, to_col = r + 1 - ap, c + 1 - bp
                direct = row_ok(to_row) & col_ok(to_col)
                if ap != 1:
                    if bp == 1:
                        continue
                    direct = direct & (c % 2 == 1 - bp // 2)

                @pl.when(direct)
                def _():
                    for a in range(3):
                        @pl.when(row_ok(to_row + a - 1))
                        def _():
                            spans(to_col, lambda first, count: fn(
                                green_copy(ap, bp, a, first, count, (to_row, to_col))))

    def each_green_received(fn):
        for ap in range(3):
            for bp in range(3):
                if bp == 1:
                    continue

                @pl.when(row_ok(r + ap - 1) & col_ok(c + bp - 1))
                def _():
                    for a in range(3):
                        @pl.when(row_ok(r + a - 1))
                        def _():
                            spans(c, lambda first, count: fn(
                                green_copy(ap, bp, a, first, count, (r, c))))

    low = 1 - c % 2 + (c < 2).astype(jnp.int32)
    rim_chip = (c < 2) | (c >= cols - 2)

    def each_staged(fn, to):
        for side in range(2):
            ap = 2 * side
            target = r + 1 - ap if to else r
            source = target + ap - 1

            @pl.when(row_ok(target) & row_ok(source))
            def _():
                for a in range(3):
                    @pl.when(row_ok(target + a - 1))
                    def _():
                        def piece(count):
                            fn(pltpu.make_async_remote_copy(
                                src_ref=green_ref.at[0, 0, :, pl.ds(
                                    at_lane(5 * (a - ap + 2) + low), count * width)],
                                dst_ref=stage.at[side, a, :, pl.ds(0, count * width)],
                                send_sem=stage_send.at[side, a],
                                recv_sem=stage_recv.at[side, a],
                                device_id=(target, c),
                                device_id_type=MESH))

                        @pl.when(rim_chip)
                        def _():
                            piece(3)

                        @pl.when(jnp.logical_not(rim_chip))
                        def _():
                            piece(4)

    def each_forwarded(fn):
        for side in range(2):
            ap = 2 * side
            for bp in (0, 2):
                sibling = c + 1 - bp

                @pl.when(row_ok(r + ap - 1) & (c % 2 == bp // 2))
                def _():
                    for a in range(3):
                        @pl.when(row_ok(r + a - 1))
                        def _():
                            spans(sibling, lambda first, count: fn(pltpu.make_async_remote_copy(
                                src_ref=stage.at[side, a, :, pl.ds(
                                    at_lane(first - bp + 2 - low), count * width)],
                                dst_ref=pairs.at[
                                    pl.ds((3 * ap + bp) * width, width),
                                    pl.ds((3 * a + first) * width, count * width)],
                                send_sem=forward_send.at[side, a],
                                recv_sem=green_recv.at[3 * ap + bp, a],
                                device_id=(r, sibling),
                                device_id_type=MESH)))

    def each_tensor_sent(step, fn):
        other = partner(step)
        for a in range(3):
            @pl.when(row_ok(other + a - 1))
            def _():
                spans(c, lambda first, count: fn(tensor_copy(r, other, step, a, first, count)))

    def each_tensor_received(step, fn):
        other = partner(step)
        for a in range(3):
            @pl.when(row_ok(r + a - 1))
            def _():
                spans(c, lambda first, count: fn(tensor_copy(other, r, step, a, first, count)))

    own = pltpu.make_async_copy(tensor_ref.at[0, r, 0], held.at[0], own_sem)
    own.start()
    own_green = []
    for a in range(3):
        band = 5 * (a + 1) + 1
        own_green.append(pltpu.make_async_copy(
            green_ref.at[0, 0, :, pl.ds(band * width, 3 * width)],
            pairs.at[pl.ds(4 * width, width), pl.ds(3 * a * width, 3 * width)],
            own_green_sem.at[a]))
        own_green[a].start()

    barrier = pltpu.get_barrier_semaphore()

    def greet(row, col):
        pl.semaphore_signal(barrier, inc=1, device_id=(row, col), device_id_type=MESH)

    @pl.loop(1, rows)
    def _(step):
        greet(partner(step), c)

    @pl.loop(1, cols)
    def _(step):
        greet(r, (c + step) % cols)

    corners = 0
    for dr in (-1, 1):
        for dc in (-1, 1):
            there = row_ok(r + dr) & col_ok(c + dc)
            corners = corners + there.astype(jnp.int32)

            @pl.when(there)
            def _():
                greet(r + dr, c + dc)

    pl.semaphore_wait(barrier, rows - 1 + cols - 1 + corners)

    @pl.loop(rows // 2, rows // 2 + 1)
    def _(step):
        each_tensor_sent(step, lambda copy: copy.start())

    each_staged(lambda copy: copy.start(), True)

    @pl.loop(rows // 2 + 1, rows // 2 + 2)
    def _(step):
        each_tensor_sent(step, lambda copy: copy.start())

    each_green_sent(lambda copy: copy.start())

    @pl.loop(rows // 2 + 2, rows)
    def _(step):
        each_tensor_sent(step, lambda copy: copy.start())

    @pl.loop(1, rows // 2)
    def _(step):
        each_tensor_sent(step, lambda copy: copy.start())

    @pl.loop(1, rows)
    def _(step):
        for a in range(3):
            for b in range(3):
                @pl.when(jnp.logical_not(row_ok(r + a - 1) & col_ok(c + b - 1)))
                def _():
                    held[step, :, pl.ds((3 * a + b) * width, width)] = jnp.zeros((width, width), held.dtype)

    for copy in own_green:
        copy.wait()
    each_staged(lambda copy: copy.wait_recv(), False)
    each_forwarded(lambda copy: copy.start())
    each_green_received(lambda copy: copy.wait_recv())

    keep = []
    for k in range(9):
        a, b = k // 3, k % 3
        inside = (row_ok(r + a - 1) & col_ok(c + b - 1)).astype(jnp.int32)
        keep.append((mask_ref[0, 0, k] == 1).astype(jnp.int32) * inside)
    for kp in range(9):
        for k in range(9):
            both = jnp.full((width, width), keep[kp] * keep[k], jnp.int32)
            if kp in (1, 7):
                block = jnp.minimum(jnp.maximum(k % 3 + 1 - low, 0), 3)
                tile = stage[kp // 6, k // 3, :, pl.ds(at_lane(block), width)]
            else:
                tile = pairs[kp * width:(kp + 1) * width, k * width:(k + 1) * width]
            tile = tile.astype(jnp.float32)
            pairs[kp * width:(kp + 1) * width, k * width:(k + 1) * width] = jnp.where(
                both == 1, tile, 0.0).astype(pairs.dtype)

    own.wait()
    occ = occ_ref[0, 0].astype(jnp.float32)

    def apply_green(start, count):
        stacked = held[pl.ds(start, count)].reshape(count * width, wide)
        for a in range(3):
            lanes = slice(3 * a * width, 3 * (a + 1) * width)
            half[pl.ds(start, count), :, lanes] = jnp.dot(
                stacked, pairs[:, lanes], preferred_element_type=jnp.float32
            ).astype(half.dtype).reshape(count, width, 3 * width)

    def pair_rows(left, left_count, right, right_count):
        gram = lax.dot_general(
            half[pl.ds(left, left_count)].reshape(left_count * width, wide),
            held[pl.ds(right, right_count)].reshape(right_count * width, wide),
            NT, preferred_element_type=jnp.float32)
        for i in range(left_count):
            for j in range(right_count):
                tile = gram[i * width:(i + 1) * width, j * width:(j + 1) * width]
                part[partner(left + i), pl.ds(partner(right + j), 1), :] = jnp.sum(
                    tile * occ, axis=0, keepdims=True)

    def arrive(step):
        each_tensor_received(step, lambda copy: copy.wait_recv())

    if rows <= 8:
        for start in range(0, rows, 2):
            for step in range(max(start, 1), start + 2):
                arrive(step)
            apply_green(start, 2)
            pair_rows(start, 2, 0, start + 2)
            if start:
                pair_rows(0, start, start, 2)
    else:
        @pl.loop(0, rows // 2)
        def _(group):
            start = 2 * group

            @pl.when(group > 0)
            def _():
                arrive(start)

            arrive(start + 1)
            apply_green(start, 2)

            @pl.loop(0, group + 1)
            def _(earlier):
                pair_rows(start, 2, 2 * earlier, 2)
                pair_rows(2 * earlier, 2, start, 2)

    row_sums[r] = jnp.zeros(row_sums.shape[1:], jnp.float32)
    row_sums[r, :, 0:rows] = jnp.sum(part[...], axis=2)

    def row_copy(step, src, dst):
        return pltpu.make_async_remote_copy(
            src_ref=row_sums.at[src], dst_ref=row_sums.at[src],
            send_sem=row_send.at[step], recv_sem=row_recv.at[step],
            device_id=(dst, c), device_id_type=MESH)

    def col_copy(step, src, dst):
        return pltpu.make_async_remote_copy(
            src_ref=col_sums.at[src], dst_ref=col_sums.at[src],
            send_sem=col_send.at[step], recv_sem=col_recv.at[step],
            device_id=(r, dst), device_id_type=MESH)

    @pl.loop(1, rows)
    def _(step):
        row_copy(step, r, partner(step)).start()

    @pl.loop(1, rows)
    def _(step):
        row_copy(step, partner(step), r).wait_recv()

    col_sums[c] = jnp.sum(row_sums[...], axis=0)

    @pl.loop(1, cols)
    def _(step):
        col_copy(step, c, (c + step) % cols).start()

    @pl.loop(1, cols)
    def _(step):
        col_copy(step, (c + cols - step) % cols, c).wait_recv()

    out_ref[...] = (jnp.sum(col_sums[...], axis=0) * scale)[:, 0:rows]

    each_green_sent(lambda copy: copy.wait_send())
    each_staged(lambda copy: copy.wait_send(), True)
    each_forwarded(lambda copy: copy.wait_send())

    @pl.loop(1, rows)
    def _(step):
        each_tensor_sent(step, lambda copy: copy.wait_send())
        row_copy(step, r, partner(step)).wait_send()

    @pl.loop(1, cols)
    def _(step):
        col_copy(step, c, (c + step) % cols).wait_send()


def per_device(tensor_ri, block_mask, green_virt, green_occ):
    rows = lax.axis_size("row")
    cols = lax.axis_size("col")
    width = green_occ.shape[-1]
    wide = tensor_ri.shape[-1]
    scale = 1.0 / math.sqrt(width * rows * cols * wide)
    lanes = 128
    hbm = pl.BlockSpec(memory_space=pltpu.MemorySpace.HBM)
    dma = pltpu.SemaphoreType.DMA
    return pl.pallas_call(
        functools.partial(kernel, rows, cols, width, scale),
        out_shape=jax.ShapeDtypeStruct((rows, rows), jnp.float32),
        in_specs=[
            pl.BlockSpec(memory_space=pltpu.MemorySpace.SMEM),
            pl.BlockSpec(memory_space=pltpu.MemorySpace.VMEM),
            hbm,
            hbm,
        ],
        out_specs=pl.BlockSpec(memory_space=pltpu.MemorySpace.VMEM),
        scratch_shapes=[
            pltpu.VMEM((rows, width, wide), jnp.bfloat16),
            pltpu.VMEM((rows, width, wide), jnp.bfloat16),
            pltpu.VMEM((wide, wide), jnp.bfloat16),
            pltpu.VMEM((2, 3, width, 4 * width), jnp.bfloat16),
            pltpu.VMEM((rows, rows, width), jnp.float32),
            pltpu.VMEM((rows, rows, lanes), jnp.float32),
            pltpu.VMEM((cols, rows, lanes), jnp.float32),
            dma,
            dma((3,)),
            dma((rows, 3)),
            dma((rows, 3)),
            dma((9, 3)),
            dma((9, 3)),
            dma((2, 3)),
            dma((2, 3)),
            dma((2, 3)),
            dma((rows,)),
            dma((rows,)),
            dma((cols,)),
            dma((cols,)),
        ],
        compiler_params=pltpu.CompilerParams(
            collective_id=0, has_side_effects=True, vmem_limit_bytes=63 * 1024 * 1024),
    )(block_mask, green_occ, tensor_ri, green_virt)


def solution(mesh):
    return jax.shard_map(
        per_device,
        mesh=mesh,
        in_specs=(
            P("row", None, "col", None, None),
            P("row", "col", None),
            P("row", "col", None, None),
            P("row", "col", None, None),
        ),
        out_specs=P(),
        check_vma=False,
    )
```

```python
import functools
import math

import jax
import jax.numpy as jnp
from jax import lax
from jax.experimental import pallas as pl
from jax.experimental.pallas import tpu as pltpu
from jax.sharding import PartitionSpec as P

MESH = pl.DeviceIdType.MESH
NT = (((1,), (1,)), ((), ()))


def kernel(rows, cols, width, scale, mask_ref, occ_ref, tensor_ref, green_ref, out_ref,
           held, half, pairs, stage, part, row_sums, col_sums,
           own_sem, own_green_sem, send_sem, recv_sem, green_send, green_recv,
           stage_send, stage_recv, forward_send,
           row_send, row_recv, col_send, col_recv):
    r = lax.axis_index("row")
    c = lax.axis_index("col")
    bits = (rows - 1).bit_length()
    wide = 9 * width

    def partner(step):
        other = 0
        for bit in range(bits):
            other = other + (1 << bit) * ((r // (1 << bit) + step // (1 << bit)) % 2)
        return other

    def at_lane(block):
        return pl.multiple_of(block * width, width)

    def spans(col, fn):
        inner = (col > 0) & (col < cols - 1)

        @pl.when(inner)
        def _():
            fn(0, 3)

        @pl.when(col == 0)
        def _():
            fn(1, 2)

        @pl.when(col == cols - 1)
        def _():
            fn(0, 2)

    def tensor_copy(src_row, dst_row, step, a, first, count):
        lanes = pl.ds((3 * a + first) * width, count * width)
        return pltpu.make_async_remote_copy(
            src_ref=tensor_ref.at[0, dst_row, 0, :, lanes],
            dst_ref=held.at[step, :, lanes],
            send_sem=send_sem.at[step, a],
            recv_sem=recv_sem.at[step, a],
            device_id=(dst_row, c),
            device_id_type=MESH,
        )

    def green_copy(ap, bp, a, first, count, target):
        slot = 3 * ap + bp
        band = 5 * (a - ap + 2) + (first - bp + 2)
        return pltpu.make_async_remote_copy(
            src_ref=green_ref.at[0, 0, :, pl.ds(band * width, count * width)],
            dst_ref=pairs.at[pl.ds(slot * width, width), pl.ds((3 * a + first) * width, count * width)],
            send_sem=green_send.at[slot, a],
            recv_sem=green_recv.at[slot, a],
            device_id=target,
            device_id_type=MESH,
        )

    def row_ok(row):
        return (row >= 0) & (row < rows)

    def col_ok(col):
        return (col >= 0) & (col < cols)

    def each_green_sent(fn):
        for ap in range(3):
            for bp in range(3):
                if ap == 1 and bp == 1:
                    continue
                to_row, to_col = r + 1 - ap, c + 1 - bp
                direct = row_ok(to_row) & col_ok(to_col)
                if ap != 1:
                    if bp == 1:
                        continue
                    direct = direct & (c % 2 == 1 - bp // 2)

                @pl.when(direct)
                def _():
                    for a in range(3):
                        @pl.when(row_ok(to_row + a - 1))
                        def _():
                            spans(to_col, lambda first, count: fn(
                                green_copy(ap, bp, a, first, count, (to_row, to_col))))

    def each_green_received(fn):
        for ap in range(3):
            for bp in range(3):
                if bp == 1:
                    continue

                @pl.when(row_ok(r + ap - 1) & col_ok(c + bp - 1))
                def _():
                    for a in range(3):
                        @pl.when(row_ok(r + a - 1))
                        def _():
                            spans(c, lambda first, count: fn(
                                green_copy(ap, bp, a, first, count, (r, c))))

    low = 1 - c % 2 + (c < 2).astype(jnp.int32)
    rim_chip = (c < 2) | (c >= cols - 2)

    def each_staged(fn, to):
        for side in range(2):
            ap = 2 * side
            target = r + 1 - ap if to else r
            source = target + ap - 1

            @pl.when(row_ok(target) & row_ok(source))
            def _():
                for a in range(3):
                    @pl.when(row_ok(target + a - 1))
                    def _():
                        def piece(count):
                            fn(pltpu.make_async_remote_copy(
                                src_ref=green_ref.at[0, 0, :, pl.ds(
                                    at_lane(5 * (a - ap + 2) + low), count * width)],
                                dst_ref=stage.at[side, a, :, pl.ds(0, count * width)],
                                send_sem=stage_send.at[side, a],
                                recv_sem=stage_recv.at[side, a],
                                device_id=(target, c),
                                device_id_type=MESH))

                        @pl.when(rim_chip)
                        def _():
                            piece(3)

                        @pl.when(jnp.logical_not(rim_chip))
                        def _():
                            piece(4)

    def each_forwarded(fn):
        for side in range(2):
            ap = 2 * side
            for bp in (0, 2):
                sibling = c + 1 - bp

                @pl.when(row_ok(r + ap - 1) & (c % 2 == bp // 2))
                def _():
                    for a in range(3):
                        @pl.when(row_ok(r + a - 1))
                        def _():
                            spans(sibling, lambda first, count: fn(pltpu.make_async_remote_copy(
                                src_ref=stage.at[side, a, :, pl.ds(
                                    at_lane(first - bp + 2 - low), count * width)],
                                dst_ref=pairs.at[
                                    pl.ds((3 * ap + bp) * width, width),
                                    pl.ds((3 * a + first) * width, count * width)],
                                send_sem=forward_send.at[side, a],
                                recv_sem=green_recv.at[3 * ap + bp, a],
                                device_id=(r, sibling),
                                device_id_type=MESH)))

    def each_tensor_sent(step, fn):
        other = partner(step)
        for a in range(3):
            @pl.when(row_ok(other + a - 1))
            def _():
                spans(c, lambda first, count: fn(tensor_copy(r, other, step, a, first, count)))

    def each_tensor_received(step, fn):
        other = partner(step)
        for a in range(3):
            @pl.when(row_ok(r + a - 1))
            def _():
                spans(c, lambda first, count: fn(tensor_copy(other, r, step, a, first, count)))

    own = pltpu.make_async_copy(tensor_ref.at[0, r, 0], held.at[0], own_sem)
    own.start()
    own_green = []
    for a in range(3):
        band = 5 * (a + 1) + 1
        own_green.append(pltpu.make_async_copy(
            green_ref.at[0, 0, :, pl.ds(band * width, 3 * width)],
            pairs.at[pl.ds(4 * width, width), pl.ds(3 * a * width, 3 * width)],
            own_green_sem.at[a]))
        own_green[a].start()

    barrier = pltpu.get_barrier_semaphore()

    def greet(row, col):
        pl.semaphore_signal(barrier, inc=1, device_id=(row, col), device_id_type=MESH)

    @pl.loop(1, rows)
    def _(step):
        greet(partner(step), c)

    @pl.loop(1, cols)
    def _(step):
        greet(r, (c + step) % cols)

    corners = 0
    for dr in (-1, 1):
        for dc in (-1, 1):
            there = row_ok(r + dr) & col_ok(c + dc)
            corners = corners + there.astype(jnp.int32)

            @pl.when(there)
            def _():
                greet(r + dr, c + dc)

    pl.semaphore_wait(barrier, rows - 1 + cols - 1 + corners)

    @pl.loop(rows // 2, rows // 2 + 1)
    def _(step):
        each_tensor_sent(step, lambda copy: copy.start())

    each_staged(lambda copy: copy.start(), True)

    @pl.loop(1, 2)
    def _(step):
        each_tensor_sent(step, lambda copy: copy.start())

    @pl.loop(rows // 2 + 1, rows // 2 + 2)
    def _(step):
        each_tensor_sent(step, lambda copy: copy.start())

    each_green_sent(lambda copy: copy.start())

    @pl.loop(2, rows // 2)
    def _(step):
        each_tensor_sent(rows // 2 + step, lambda copy: copy.start())
        each_tensor_sent(step, lambda copy: copy.start())

    @pl.loop(1, rows)
    def _(step):
        for a in range(3):
            for b in range(3):
                @pl.when(jnp.logical_not(row_ok(r + a - 1) & col_ok(c + b - 1)))
                def _():
                    held[step, :, pl.ds((3 * a + b) * width, width)] = jnp.zeros((width, width), held.dtype)

    for copy in own_green:
        copy.wait()
    each_staged(lambda copy: copy.wait_recv(), False)
    each_forwarded(lambda copy: copy.start())
    each_green_received(lambda copy: copy.wait_recv())

    keep = []
    for k in range(9):
        a, b = k // 3, k % 3
        inside = (row_ok(r + a - 1) & col_ok(c + b - 1)).astype(jnp.int32)
        keep.append((mask_ref[0, 0, k] == 1).astype(jnp.int32) * inside)
    for kp in range(9):
        for k in range(9):
            both = jnp.full((width, width), keep[kp] * keep[k], jnp.int32)
            if kp in (1, 7):
                block = jnp.minimum(jnp.maximum(k % 3 + 1 - low, 0), 3)
                tile = stage[kp // 6, k // 3, :, pl.ds(at_lane(block), width)]
            else:
                tile = pairs[kp * width:(kp + 1) * width, k * width:(k + 1) * width]
            tile = tile.astype(jnp.float32)
            pairs[kp * width:(kp + 1) * width, k * width:(k + 1) * width] = jnp.where(
                both == 1, tile, 0.0).astype(pairs.dtype)

    own.wait()
    occ = occ_ref[0, 0].astype(jnp.float32)

    def apply_green(start, count):
        stacked = held[pl.ds(start, count)].reshape(count * width, wide)
        for a in range(3):
            lanes = slice(3 * a * width, 3 * (a + 1) * width)
            half[pl.ds(start, count), :, lanes] = jnp.dot(
                stacked, pairs[:, lanes], preferred_element_type=jnp.float32
            ).astype(half.dtype).reshape(count, width, 3 * width)

    def pair_rows(left, left_count, right, right_count):
        gram = lax.dot_general(
            half[pl.ds(left, left_count)].reshape(left_count * width, wide),
            held[pl.ds(right, right_count)].reshape(right_count * width, wide),
            NT, preferred_element_type=jnp.float32)
        for i in range(left_count):
            for j in range(right_count):
                tile = gram[i * width:(i + 1) * width, j * width:(j + 1) * width]
                part[partner(left + i), pl.ds(partner(right + j), 1), :] = jnp.sum(
                    tile * occ, axis=0, keepdims=True)

    def arrive(step):
        each_tensor_received(step, lambda copy: copy.wait_recv())

    if rows <= 8:
        for start in range(0, rows, 2):
            for step in range(max(start, 1), start + 2):
                arrive(step)
            apply_green(start, 2)
            pair_rows(start, 2, 0, start + 2)
            if start:
                pair_rows(0, start, start, 2)
    else:
        @pl.loop(0, rows // 2)
        def _(group):
            start = 2 * group

            @pl.when(group > 0)
            def _():
                arrive(start)

            arrive(start + 1)
            apply_green(start, 2)

            @pl.loop(0, group + 1)
            def _(earlier):
                pair_rows(start, 2, 2 * earlier, 2)
                pair_rows(2 * earlier, 2, start, 2)

    row_sums[r] = jnp.zeros(row_sums.shape[1:], jnp.float32)
    row_sums[r, :, 0:rows] = jnp.sum(part[...], axis=2)

    def row_copy(step, src, dst):
        return pltpu.make_async_remote_copy(
            src_ref=row_sums.at[src], dst_ref=row_sums.at[src],
            send_sem=row_send.at[step], recv_sem=row_recv.at[step],
            device_id=(dst, c), device_id_type=MESH)

    def col_copy(step, src, dst):
        return pltpu.make_async_remote_copy(
            src_ref=col_sums.at[src], dst_ref=col_sums.at[src],
            send_sem=col_send.at[step], recv_sem=col_recv.at[step],
            device_id=(r, dst), device_id_type=MESH)

    @pl.loop(1, rows)
    def _(step):
        row_copy(step, r, partner(step)).start()

    @pl.loop(1, rows)
    def _(step):
        row_copy(step, partner(step), r).wait_recv()

    col_sums[c] = jnp.sum(row_sums[...], axis=0)

    @pl.loop(1, cols)
    def _(step):
        col_copy(step, c, (c + step) % cols).start()

    @pl.loop(1, cols)
    def _(step):
        col_copy(step, (c + cols - step) % cols, c).wait_recv()

    out_ref[...] = (jnp.sum(col_sums[...], axis=0) * scale)[:, 0:rows]

    each_green_sent(lambda copy: copy.wait_send())
    each_staged(lambda copy: copy.wait_send(), True)
    each_forwarded(lambda copy: copy.wait_send())

    @pl.loop(1, rows)
    def _(step):
        each_tensor_sent(step, lambda copy: copy.wait_send())
        row_copy(step, r, partner(step)).wait_send()

    @pl.loop(1, cols)
    def _(step):
        col_copy(step, c, (c + step) % cols).wait_send()


def per_device(tensor_ri, block_mask, green_virt, green_occ):
    rows = lax.axis_size("row")
    cols = lax.axis_size("col")
    width = green_occ.shape[-1]
    wide = tensor_ri.shape[-1]
    scale = 1.0 / math.sqrt(width * rows * cols * wide)
    lanes = 128
    hbm = pl.BlockSpec(memory_space=pltpu.MemorySpace.HBM)
    dma = pltpu.SemaphoreType.DMA
    return pl.pallas_call(
        functools.partial(kernel, rows, cols, width, scale),
        out_shape=jax.ShapeDtypeStruct((rows, rows), jnp.float32),
        in_specs=[
            pl.BlockSpec(memory_space=pltpu.MemorySpace.SMEM),
            pl.BlockSpec(memory_space=pltpu.MemorySpace.VMEM),
            hbm,
            hbm,
        ],
        out_specs=pl.BlockSpec(memory_space=pltpu.MemorySpace.VMEM),
        scratch_shapes=[
            pltpu.VMEM((rows, width, wide), jnp.bfloat16),
            pltpu.VMEM((rows, width, wide), jnp.bfloat16),
            pltpu.VMEM((wide, wide), jnp.bfloat16),
            pltpu.VMEM((2, 3, width, 4 * width), jnp.bfloat16),
            pltpu.VMEM((rows, rows, width), jnp.float32),
            pltpu.VMEM((rows, rows, lanes), jnp.float32),
            pltpu.VMEM((cols, rows, lanes), jnp.float32),
            dma,
            dma((3,)),
            dma((rows, 3)),
            dma((rows, 3)),
            dma((9, 3)),
            dma((9, 3)),
            dma((2, 3)),
            dma((2, 3)),
            dma((2, 3)),
            dma((rows,)),
            dma((rows,)),
            dma((cols,)),
            dma((cols,)),
        ],
        compiler_params=pltpu.CompilerParams(
            collective_id=0, has_side_effects=True, vmem_limit_bytes=63 * 1024 * 1024),
    )(block_mask, green_occ, tensor_ri, green_virt)


def solution(mesh):
    return jax.shard_map(
        per_device,
        mesh=mesh,
        in_specs=(
            P("row", None, "col", None, None),
            P("row", "col", None),
            P("row", "col", None, None),
            P("row", "col", None, None),
        ),
        out_specs=P(),
        check_vma=False,
    )
```
